32 devices in a mesh: pop: 2 (over x), dp: 8 (over z, y), tp: 2 (over core).
Axes of the slice: x: 2, y: 2, z: 4, core: 2. Of those that a mesh axis runs over, the one named last changes fastest.
Arguments:
- q_latent: bfloat16 [256, 128, 512], P(('pop', 'dp')), parts along dimension 0
- q_rope: bfloat16 [256, 8192], P(('pop', 'dp')), parts along dimension 0
- new_entry: bfloat16 [256, 576], P(('pop', 'dp')), parts along dimension 0
- cache_latent: bfloat16 [768, 64, 512], P(('pop', 'dp'), 'tp'), parts along dimension 0, may hold values from -6 to 6
- cache_rope: bfloat16 [768, 4096], P(('pop', 'dp'), 'tp'), parts along dimension 0, may hold values from -6 to 6
- source_rank: int32 [256, 16, 1], P(('pop', 'dp')), parts along dimension 0, may hold values from 0 to 7; in each aligned block of 256 rows (0 to 255, 256 to 511, ..., all dimensions but the last counted through in order) at most 40 rows name the same one
- slot_index: int32 [256, 16], P(('pop', 'dp')), parts along dimension 0, may hold values from 0 to 47
- lengths: int32 [256], P(('pop', 'dp')), parts along dimension 0, may hold values from 897 to 1024, as said below
- value_up_weight: bfloat16 [128, 512, 128], P('tp'), may hold values from -0.25 to 0.25
Outputs:
- attn_out: bfloat16 [256, 16384], P(('pop', 'dp'), 'tp'), parts along dimension 0
The draws below stay inside these ranges and needn't reach their ends.
There are 2 independent parts, one for each index of `pop`. The reference program is written for one: setup_inputs(seed, part) draws one part's arguments, and reference() takes and returns one part's arrays. A program takes and returns all parts, laid end to end along the dimension named above; an argument that names none is the same for every part. Nothing has to cross between parts.
Inputs may be any that keep to these rules, and one draw needn't show every extreme that they name: `source_rank`: within the table rows of the 16 requests of one dp rank, no source rank is named more than 40 times; in some ranks' rows one source rank is named exactly 40 times. `lengths`: some request has the full length 1024.
All inputs are finite; a program needn't handle non-finite values.
Results may differ from the reference program's by a relative error of at most 0.0052.
Values may be sent and summed in bfloat16 or wider, within the bound.
A program may use at most 128 MiB of HBM per device.

```python
import math
import jax
import jax.numpy as jnp
import numpy as np
from jax import lax

H = 128
KVL = 512
RD = 64
VD = 128
BLK = 64
R_DEV = 16
MAXB = 16
SLOTS_DEV = 48
REQ = 128
POOL = 384
CAP = 40
N_DP = 8
N_TP = 2


def fresh_entry(key):
    base_key = jax.random.fold_in(key, 101)
    return jax.random.normal(base_key, (REQ, KVL + RD), jnp.float32)


def draw_new_entry(key, part):
    return fresh_entry(key).astype(jnp.bfloat16)


def draw_q_latent(key, part):
    own_key = jax.random.fold_in(key, 202)
    return jax.random.normal(own_key, (REQ, H, KVL), jnp.float32).astype(jnp.bfloat16)


def draw_q_rope(key, part):
    own_key = jax.random.fold_in(key, 303)
    return jax.random.normal(own_key, (REQ, H * RD), jnp.float32).astype(jnp.bfloat16)


def draw_lengths(key, part):
    raw_len = jax.random.randint(jax.random.fold_in(key, 2), (REQ,), 0, 2 * BLK)
    draw_len = (MAXB - 2) * BLK + 1 + raw_len
    chosen = jax.random.randint(jax.random.fold_in(key, 3), (), 0, REQ)
    return draw_len.at[chosen].set(MAXB * BLK).astype(jnp.int32)


def touch_ends(values, rng, low, largest):
    longest = values.shape.index(max(values.shape))
    spots = []
    for shift in (0, 1):
        where = [jax.random.randint(jax.random.fold_in(rng, axis), (), 0, length) for axis, length in enumerate(values.shape)]
        where[longest] = (where[longest] + shift) % values.shape[longest]
        spots.append(tuple(where))
    return values.at[spots[0]].set(low).at[spots[1]].set(largest)


def block_scale(rng, shape, split, least, largest):
    def one(axis_at, blocks):
        steps = jax.random.uniform(jax.random.fold_in(jax.random.fold_in(rng, 6), axis_at), (blocks,), jnp.float32, least / len(split), largest / len(split))
        return jnp.repeat(jnp.exp(steps), shape[axis_at] // blocks).reshape((-1,) + (1,) * (len(shape) - axis_at - 1))

    gain = one(*split[0])
    for cut in split[1:]:
        gain = gain * one(*cut)
    return gain


def deal_out(stream_key, own, number, rows, number_of, top, bound, slope):
    sequence = jax.random.permutation(stream_key, number_of)
    heavy_load, ordinary = shares(number_of, rows * top, bound, slope, True), shares(number_of, rows * top, bound, slope, False)
    places = jnp.arange(number_of)

    def named(tallies, offset_by):
        used = int((tallies > 0).sum())
        fixed = max(1, used // 4)
        moved = fixed + (places - fixed + offset_by * (used - fixed)) % max(1, number_of - fixed)
        return jnp.zeros((number_of,), jnp.int32).at[sequence[jnp.where(places < fixed, places, moved)]].set(jnp.asarray(tallies, jnp.int32))

    tallies = jnp.where(number % 4 == 0, named(heavy_load, number // 4), named(ordinary, number - number // 4 - 1))
    mixed = jax.random.permutation(jax.random.fold_in(own, 3), number_of)
    giver, sink = mixed[0:number_of // 2 * 2:2], mixed[1:number_of // 2 * 2:2]
    room = jnp.minimum(tallies[giver] - 1, bound - tallies[sink]) // 2
    room = jnp.where((giver == sequence[0]) | (sink == sequence[0]) | (tallies[sink] == 0), 0, jnp.maximum(room, 0))
    moved = jax.random.randint(jax.random.fold_in(own, 4), (number_of // 2,), 0, 1 << 20) % (room + 1)
    tallies = tallies.at[giver].add(-moved).at[sink].add(moved)
    members = jnp.searchsorted(jnp.cumsum(tallies), jnp.arange(rows * top), side="right").astype(jnp.int32)
    table = members.reshape(top, rows).T
    table = table[jax.random.permutation(jax.random.fold_in(own, 1), rows)]
    offset_by = jax.random.randint(jax.random.fold_in(own, 2), (rows, 1), 0, top)
    return jnp.take_along_axis(table, (jnp.arange(top)[None, :] + offset_by) % top, axis=1)


def shares(number_of, total, bound, skew, full):
    loads = [(1 << 20) // math.isqrt(rank ** skew) + 1 for rank in range(1, number_of + 1)]
    largest = bound if full else min(bound, max(-(-total // number_of), total * loads[0] // sum(loads)))
    least = 1 if total - largest >= number_of - 1 else 0
    counts, rest = [largest] + [least] * (number_of - 1), total - largest - least * (number_of - 1)
    while rest > 0:
        free = [i for i in range(1, number_of) if counts[i] < largest] or [i for i in range(1, number_of) if counts[i] < bound]
        whole, remaining = sum([loads[i] for i in free]), rest
        for i in free:
            addition = min(bound - counts[i], max(1, remaining * loads[i] // whole), rest)
            counts[i] = counts[i] + addition
            rest = rest - addition
    return np.array(counts)


def normal_values(rng, shape, deviation, most, shards=(), kind=jnp.bfloat16):
    values = jax.random.normal(rng, shape, jnp.float32) * deviation
    if len(shards) > 0:
        values = block_scale(rng, shape, shards, -0.22, 0.18) * values
    return jnp.clip(values, min=-most, max=most).astype(kind)


def setup_inputs(seed: int = 0, part: int = 0) -> dict:
    arg_keys = jax.random.split(jax.random.key(seed), 10)
    own_keys = jax.random.split(jax.random.fold_in(arg_keys[9], part), 10)
    q_latent = draw_q_latent(jax.random.fold_in(jax.random.fold_in(arg_keys[9], part), 71), part)
    q_rope = draw_q_rope(jax.random.fold_in(jax.random.fold_in(arg_keys[9], part), 71), part)
    new_entry = draw_new_entry(jax.random.fold_in(jax.random.fold_in(arg_keys[9], part), 71), part)
    cache_latent = normal_values(own_keys[3], (POOL, BLK, KVL), 1.0, 6.0, ((0, 8), (1, 2)))
    cache_rope = normal_values(own_keys[4], (POOL, BLK * RD), 1.0, 6.0, ((0, 8), (1, 2)))
    source_rank_keys = jax.random.split(jax.random.fold_in(own_keys[5], 1), REQ * MAXB // (R_DEV * MAXB))
    source_rank_turns = jax.random.permutation(jax.random.fold_in(own_keys[5], 3), REQ * MAXB // (R_DEV * MAXB))
    source_rank = jax.vmap(lambda own, number: deal_out(jax.random.fold_in(own_keys[5], 2), own, number, R_DEV * MAXB, N_DP, 1, CAP, 2))(source_rank_keys, source_rank_turns).reshape((REQ, MAXB, 1))
    slot_index = touch_ends(jax.random.randint(own_keys[6], (REQ, MAXB), 0, SLOTS_DEV), jax.random.fold_in(own_keys[6], 1), 0, SLOTS_DEV - 1).astype(jnp.int32)
    lengths = draw_lengths(jax.random.fold_in(jax.random.fold_in(arg_keys[9], part), 71), part)
    value_up_weight = normal_values(arg_keys[8], (H, KVL, VD), KVL ** -0.5, 0.25, ((0, 2),))
    return {"q_latent": q_latent, "q_rope": q_rope, "new_entry": new_entry, "cache_latent": cache_latent, "cache_rope": cache_rope, "source_rank": source_rank, "slot_index": slot_index, "lengths": lengths, "value_up_weight": value_up_weight}


softmax_scale = 192.0 ** -0.5
neg_fill = -1e30


def round_bf16(values):
    return lax.optimization_barrier(values.astype(jnp.bfloat16)).astype(jnp.float32)


def reference(q_latent, q_rope, new_entry, cache_latent, cache_rope, source_rank, slot_index, lengths, value_up_weight):
    run_count = N_TP
    run_len = BLK // run_count
    slot_ids = (source_rank[:, :, 0] * SLOTS_DEV + slot_index).astype(jnp.int32)
    offsets = jnp.arange(BLK, dtype=jnp.int32)
    run_of = offsets // run_len
    positions = jnp.arange(MAXB, dtype=jnp.int32)[:, None] * BLK + offsets[None, :]
    up_projection_weight = value_up_weight.astype(jnp.float32)

    def per_request(item_tuple):
        query_lat, query_rot, own_key, slot_row, length = item_tuple
        keys_lat = cache_latent[slot_row].astype(jnp.float32)
        keys_rot = cache_rope[slot_row].reshape(MAXB, BLK, RD).astype(jnp.float32)
        qlat = query_lat.astype(jnp.float32)
        qrot = query_rot.reshape(H, RD).astype(jnp.float32)
        scores = (jnp.einsum("hk,jpk->hjp", qlat, keys_lat) + jnp.einsum("hd,jpd->hjp", qrot, keys_rot)) * softmax_scale
        own_vals = own_key.astype(jnp.float32)
        new_score = (qlat @ own_vals[:KVL] + qrot @ own_vals[KVL:]) * softmax_scale
        in_range = positions < length
        maxima = []
        numerators = []
        denominators = []
        for run_index in range(run_count):
            selected = (in_range & (run_of == run_index)[None, :])[None, :, :]
            top_score = jnp.max(jnp.where(selected, scores, neg_fill), axis=(1, 2))
            if run_index == 0:
                top_score = jnp.maximum(top_score, new_score)
            expo = jnp.where(selected, jnp.exp(scores - top_score[:, None, None]), 0.0)
            numerator = jnp.einsum("hjp,jpk->hk", round_bf16(expo), keys_lat)
            denominator = jnp.sum(expo, axis=(1, 2))
            if run_index == 0:
                incoming_token_weight = jnp.exp(new_score - top_score)
                numerator = numerator + round_bf16(incoming_token_weight)[:, None] * own_vals[None, :KVL]
                denominator = denominator + incoming_token_weight
            maxima.append(top_score)
            numerators.append(numerator)
            denominators.append(denominator)
        overall = maxima[0]
        for top_score in maxima[1:]:
            overall = jnp.maximum(overall, top_score)
        total_num = jnp.zeros((H, KVL), jnp.float32)
        total_den = jnp.zeros((H,), jnp.float32)
        for run_index in range(run_count):
            factor = jnp.exp(maxima[run_index] - overall)
            total_num = total_num + factor[:, None] * numerators[run_index]
            total_den = total_den + factor * denominators[run_index]
        latent_output_rows = round_bf16(total_num / total_den[:, None])
        value_projected_output = jnp.einsum("en,enp->ep", latent_output_rows, up_projection_weight)
        return value_projected_output.reshape(H * VD).astype(jnp.bfloat16)

    return lax.map(per_request, (q_latent, q_rope, new_entry, slot_ids, lengths))
```

```python
import functools

import jax
import jax.numpy as jnp
from jax import lax
from jax.experimental import pallas as pl
from jax.experimental.pallas import tpu as pltpu
from jax.sharding import PartitionSpec as P

softmax_scale = 192.0 ** (-0.5)
neg_fill = -1e30


def entry_places(src_flat, rank_count):
    onehot = (src_flat[:, None] == jnp.arange(rank_count, dtype=jnp.int32)[None, :]).astype(
        jnp.int32
    )
    before = jnp.cumsum(onehot, axis=0) - onehot
    return jnp.sum(before * onehot, axis=1)


def spread_local(
    q_latent,
    q_rope,
    new_entry,
    cache_latent,
    cache_rope,
    source_rank,
    slot_index,
    lengths,
    value_up_weight,
):
    rank_count = lax.axis_size("dp")
    lane_count = lax.axis_size("tp")
    my_lane = lax.axis_index("tp")
    requests, max_blocks = slot_index.shape
    run_len = cache_latent.shape[1]
    latent_dim = cache_latent.shape[2]
    heads = q_latent.shape[1]
    rope_dim = q_rope.shape[1] // heads
    entries = requests * max_blocks
    capacity = max(2, (entries * 5 + 4 * rank_count - 1) // (4 * rank_count))
    src_flat = source_rank.reshape(entries)
    slot_flat = slot_index.reshape(entries)
    places = entry_places(src_flat, rank_count)
    wanted = jnp.zeros((rank_count, capacity), jnp.int32).at[src_flat, places].set(slot_flat)
    asked_slots = lax.all_to_all(wanted, "dp", split_axis=0, concat_axis=0, tiled=True)
    send_latent = jnp.take(cache_latent, asked_slots, axis=0)
    send_rope = jnp.take(cache_rope, asked_slots, axis=0)
    got_latent, received_rotary_keys = (
        lax.all_to_all(send_latent, "dp", split_axis=0, concat_axis=0, tiled=True),
        lax.all_to_all(send_rope, "dp", split_axis=0, concat_axis=0, tiled=True),
    )
    where_from = src_flat * capacity + places
    keys_latent = jnp.take(
        got_latent.reshape(rank_count * capacity, run_len, latent_dim), where_from, axis=0
    )
    keys_latent = keys_latent.reshape(requests, max_blocks * run_len, latent_dim)
    keys_rope = jnp.take(
        received_rotary_keys.reshape(rank_count * capacity, run_len * rope_dim), where_from, axis=0
    )
    keys_rope = keys_rope.reshape(requests, max_blocks * run_len, rope_dim)
    query_rope = q_rope.reshape(requests, heads, rope_dim)
    scores = jnp.einsum("rhk,rnk->rhn", q_latent, keys_latent, preferred_element_type=jnp.float32)
    scores = (
        scores
        + jnp.einsum("rhd,rnd->rhn", query_rope, keys_rope, preferred_element_type=jnp.float32)
    ) * softmax_scale
    new_latent = new_entry[:, :latent_dim]
    incoming_rotary_key = new_entry[:, latent_dim:]
    new_score = jnp.einsum("rhk,rk->rh", q_latent, new_latent, preferred_element_type=jnp.float32)
    new_score = (
        new_score
        + jnp.einsum(
            "rhd,rd->rh", query_rope, incoming_rotary_key, preferred_element_type=jnp.float32
        )
    ) * softmax_scale
    slot_pos = jnp.arange(max_blocks * run_len, dtype=jnp.int32)
    positions = (
        slot_pos // run_len * (run_len * lane_count) + my_lane * run_len + slot_pos % run_len
    )
    in_range = (positions[None, :] < lengths[:, None])[:, None, :]
    is_first = my_lane == 0
    top_score = jnp.max(jnp.where(in_range, scores, neg_fill), axis=2)
    top_score = jnp.where(is_first, jnp.maximum(top_score, new_score), top_score)
    expo = jnp.where(in_range, jnp.exp(scores - top_score[:, :, None]), 0.0)
    numerator = jnp.einsum(
        "rhn,rnk->rhk", expo.astype(jnp.bfloat16), keys_latent, preferred_element_type=jnp.float32
    )
    denominator = jnp.sum(expo, axis=2)
    incoming_token_weight = jnp.where(is_first, jnp.exp(new_score - top_score), 0.0)
    numerator = (
        numerator
        + incoming_token_weight.astype(jnp.bfloat16).astype(jnp.float32)[:, :, None]
        * new_latent.astype(jnp.float32)[:, None, :]
    )
    denominator = denominator + incoming_token_weight
    overall = lax.pmax(top_score, "tp")
    factor = jnp.exp(top_score - overall)
    numer_sum, denom_sum = (
        lax.psum_scatter(numerator * factor[:, :, None], "tp", scatter_dimension=1, tiled=True),
        lax.psum_scatter(denominator * factor, "tp", scatter_dimension=1, tiled=True),
    )
    latent_output_rows = (numer_sum / denom_sum[:, :, None]).astype(jnp.bfloat16)
    value_projected_output = jnp.einsum(
        "wyc,yca->wya", latent_output_rows, value_up_weight, preferred_element_type=jnp.float32
    )
    return value_projected_output.reshape(requests, -1).astype(jnp.bfloat16)


MESH = pl.DeviceIdType.MESH
up, down, across = 0, 1, 2
chunk_count = 12
vmem_pool_limit = 24 * 1024 * 1024


def dot_nt(a, b):
    return lax.dot_general(a, b, (((1,), (1,)), ((), ())), preferred_element_type=jnp.float32)


def fused_kernel(
    depth,
    width,
    early,
    table,
    lengths,
    latent_hbm,
    rope_hbm,
    q_hbm,
    value_hbm,
    q_rope,
    fresh,
    out,
    latent,
    rope,
    q_latent,
    value,
    keys,
    rope_keys,
    part,
    other,
    merged,
    local_sem,
    send_sem,
    recv_sem,
    pair_send,
    pair_recv,
):
    me = lax.axis_index("dp")
    lane = lax.axis_index("tp")
    z, y = me // width, me % width
    slots = latent_hbm.shape[0]
    run_len = latent_hbm.shape[1]
    latent_dim = latent_hbm.shape[2]
    requests, heads = q_hbm.shape[0], q_hbm.shape[1]
    rope_dim = q_rope.shape[2]
    max_blocks = table.shape[0] // requests
    half = run_len // 2
    own_heads = heads // 2
    chunk = slots // chunk_count
    has_up, has_down = z + 1 < depth, z > 0

    own = pl.ds(me * slots, slots)
    local_copies = [
        pltpu.make_async_copy(latent_hbm, latent.at[own], local_sem.at[0]),
        pltpu.make_async_copy(rope_hbm, rope.at[own], local_sem.at[1]),
        pltpu.make_async_copy(q_hbm, q_latent, local_sem.at[2]),
        pltpu.make_async_copy(value_hbm, value, local_sem.at[3]),
    ]
    local_copies[0].start()
    local_copies[1].start()

    barrier = pltpu.get_barrier_semaphore()

    def greet(target):
        pl.semaphore_signal(barrier, inc=1, device_id=target, device_id_type=MESH)

    greet({"tp": 1 - lane})
    pl.when(has_up)(lambda: greet({"dp": me + width}))
    pl.when(has_down)(lambda: greet({"dp": me - width}))
    neighbours = 1 + has_up.astype(jnp.int32) + has_down.astype(jnp.int32)
    if width == 2:
        greet({"dp": z * width + 1 - y})
        neighbours = neighbours + 1
    pl.semaphore_wait(barrier, neighbours)
    local_copies[0].wait()
    local_copies[1].wait()

    def piece(origin, c, way):
        target = {up: me + width, down: me - width, across: z * width + 1 - y}[way]
        rows = pl.ds(origin * slots + c * chunk, chunk)
        return [
            pltpu.make_async_remote_copy(
                src_ref=array.at[rows],
                dst_ref=array.at[rows],
                send_sem=send_sem.at[n, way, origin, c],
                recv_sem=recv_sem.at[n, origin, c],
                device_id={"dp": target},
                device_id_type=MESH,
            )
            for n, array in enumerate((latent, rope))
        ]

    def send(origin, c, way):
        for copy in piece(origin, c, way):
            copy.start()

    def arrive(origin, c):
        for copy in piece(origin, c, up):
            copy.wait_recv()

    def sent(origin, c, way):
        for copy in piece(origin, c, way):
            copy.wait_send()

    def over(first, last, body):
        def step(c, carry):
            body(c)
            return carry

        lax.fori_loop(first, last, step, 0)

    late = (early, chunk_count)

    def own_first(c):
        pl.when(has_up)(lambda: send(me, c, up))
        pl.when(has_down)(lambda: send(me, c, down))
        if width == 2:
            send(me, c, across)

    if width == 2:
        over(0, early, lambda c: send(me, c, across))
    over(*late, own_first)
    local_copies[2].start()
    local_copies[3].start()

    def pass_on(t, columns, first, last, cross):
        def body(c):
            for column in columns:

                @pl.when(z >= t)
                def _():
                    origin = (z - t) * width + column
                    arrive(origin, c)
                    pl.when(has_up)(lambda: send(origin, c, up))
                    if cross:
                        send(origin, c, across)

                @pl.when(z + t < depth)
                def _():
                    origin = (z + t) * width + column
                    arrive(origin, c)
                    pl.when(has_down)(lambda: send(origin, c, down))
                    if cross:
                        send(origin, c, across)

        over(first, last, body)

    for t in range(1, depth):
        pass_on(t, (y,), *late, width == 2)

    if early:

        def own_last(c):
            partner = z * width + 1 - y
            arrive(partner, c)
            for origin in (me, partner):
                pl.when(has_up)(lambda: send(origin, c, up))
                pl.when(has_down)(lambda: send(origin, c, down))

        over(0, early, own_last)
        for t in range(1, depth):
            pass_on(t, (0, 1), 0, early, False)

    if width == 2:
        order = [(z + t) % depth for t in range(depth)]
        for place in order:
            over(*late, lambda c: arrive(place * width + 1 - y, c))

    local_copies[2].wait()
    local_copies[3].wait()

    def pair_copy(r):
        return pltpu.make_async_remote_copy(
            src_ref=part.at[r, pl.ds((1 - lane) * own_heads, own_heads)],
            dst_ref=other.at[r],
            send_sem=pair_send.at[r],
            recv_sem=pair_recv.at[r],
            device_id={"tp": 1 - lane},
            device_id_type=MESH,
        )

    count = max_blocks * run_len
    spot = lax.broadcasted_iota(jnp.int32, (heads, count), 1)
    in_half = spot % (count // 2)
    positions = (
        in_half // half * (2 * run_len) + lane * run_len + spot // (count // 2) * half + in_half % half
    )
    is_first = lane == 0
    stat_lane = lax.broadcasted_iota(jnp.int32, (heads, 128), 1)

    def attend(r, carry):
        side = r % 2
        pl.when(r > 0)(lambda: pair_copy(r - 1).start())
        for j in range(max_blocks):
            block = table[r * max_blocks + j]
            low = pl.ds(j * half, half)
            keys[side, low, :] = latent[block, 0:half, :]
            keys[side, pl.ds(count // 2 + j * half, half), :] = latent[block, half:run_len, :]
            rope_keys[side, low, :] = rope[block]
        q = q_latent[r]
        q_rot = q_rope[r]
        zero = jnp.zeros_like(q_rot)
        rot = rope_keys[side]
        all_keys = keys[side]
        scores = dot_nt(q, all_keys)
        low_scores = dot_nt(jnp.concatenate([q_rot, zero], axis=1), rot)
        high_scores = dot_nt(jnp.concatenate([zero, q_rot], axis=1), rot)
        scores = (scores + jnp.concatenate([low_scores, high_scores], axis=1)) * softmax_scale
        new = fresh[pl.ds(r, 1), :]
        new_latent = new[:, :latent_dim]
        new_score = jnp.sum(q.astype(jnp.float32) * new_latent, axis=1, keepdims=True)
        new_score = new_score + jnp.sum(
            q_rot.astype(jnp.float32) * new[:, latent_dim : latent_dim + rope_dim], axis=1, keepdims=True
        )
        new_score = new_score * softmax_scale
        in_range = positions < lengths[r]
        top = jnp.max(jnp.where(in_range, scores, neg_fill), axis=1, keepdims=True)
        top = jnp.where(is_first, jnp.maximum(top, new_score), top)
        expo = jnp.where(in_range, jnp.exp(scores - top), 0.0)
        weight = jnp.where(is_first, jnp.exp(new_score - top), 0.0)
        den = jnp.sum(expo, axis=1, keepdims=True) + weight
        num = jnp.dot(expo.astype(jnp.bfloat16), all_keys, preferred_element_type=jnp.float32)
        num = num + weight.astype(jnp.bfloat16).astype(jnp.float32) * new_latent
        part[r, :, 0:latent_dim] = num
        part[r, :, latent_dim : latent_dim + 128] = jnp.where(stat_lane < 64, top, den)
        return carry

    lax.fori_loop(0, requests, attend, 0)
    pair_copy(requests - 1).start()

    def merge(r, carry):
        pair_copy(r).wait_recv()
        a = part[r, pl.ds(pl.multiple_of(lane * own_heads, own_heads), own_heads), :]
        b = other[r]
        top_a, top_b = a[:, latent_dim : latent_dim + 1], b[:, latent_dim : latent_dim + 1]
        den_a, den_b = a[:, latent_dim + 64 : latent_dim + 65], b[:, latent_dim + 64 : latent_dim + 65]
        top = jnp.maximum(top_a, top_b)
        f_a, f_b = jnp.exp(top_a - top), jnp.exp(top_b - top)
        total = a[:, :latent_dim] * f_a + b[:, :latent_dim] * f_b
        merged[r] = total / (den_a * f_a + den_b * f_b)
        return carry

    lax.fori_loop(0, requests, merge, 0)

    value_dim = value.shape[2]

    def project(h, carry):
        rows = merged[:, pl.ds(h, 1), :].reshape(requests, latent_dim).astype(jnp.bfloat16)
        done = jnp.dot(rows, value[h], preferred_element_type=jnp.float32)
        out[:, pl.ds(pl.multiple_of(h * value_dim, value_dim), value_dim)] = done.astype(out.dtype)
        return carry

    lax.fori_loop(0, own_heads, project, 0)

    for place in range(depth):
        mine = place * width + y

        @pl.when(jnp.logical_and(place <= z, has_up))
        def _():
            over(*late, lambda c: sent(mine, c, up))
            for column in range(width) if early else ():
                over(0, early, lambda c: sent(place * width + column, c, up))

        @pl.when(jnp.logical_and(place >= z, has_down))
        def _():
            over(*late, lambda c: sent(mine, c, down))
            for column in range(width) if early else ():
                over(0, early, lambda c: sent(place * width + column, c, down))

        if width == 2:
            over(*late, lambda c: sent(mine, c, across))
    if early:
        over(0, early, lambda c: sent(me, c, across))

    def finish(r, carry):
        pair_copy(r).wait_send()
        return carry

    lax.fori_loop(0, requests, finish, 0)


def fused_local(
    q_latent,
    q_rope,
    new_entry,
    cache_latent,
    cache_rope,
    source_rank,
    slot_index,
    lengths,
    value_up_weight,
):
    rank_count = lax.axis_size("dp")
    width = 2 if rank_count % 2 == 0 else 1
    depth = rank_count // width
    early = chunk_count // 6 if width == 2 else 0
    requests, max_blocks = slot_index.shape
    slots, run_len, latent_dim = cache_latent.shape
    heads = q_latent.shape[1]
    rope_dim = q_rope.shape[1] // heads
    own_heads, _, value_dim = value_up_weight.shape
    half = run_len // 2
    table = (source_rank.reshape(requests, max_blocks) * slots + slot_index).reshape(-1)
    rope_pairs = (
        cache_rope.reshape(slots, 2, half, rope_dim)
        .transpose(0, 2, 1, 3)
        .reshape(slots, half, 2 * rope_dim)
    )
    count = max_blocks * run_len
    bf16, f32 = jnp.bfloat16, jnp.float32
    smem = pl.BlockSpec(memory_space=pltpu.SMEM)
    vmem = pl.BlockSpec(memory_space=pltpu.VMEM)
    anywhere = pl.BlockSpec(memory_space=pl.ANY)
    return pl.pallas_call(
        functools.partial(fused_kernel, depth, width, early),
        out_shape=jax.ShapeDtypeStruct((requests, own_heads * value_dim), bf16),
        in_specs=[smem, smem, anywhere, anywhere, anywhere, anywhere, vmem, vmem],
        out_specs=vmem,
        scratch_shapes=[
            pltpu.VMEM((rank_count * slots, run_len, latent_dim), bf16),
            pltpu.VMEM((rank_count * slots, half, 2 * rope_dim), bf16),
            pltpu.VMEM((requests, heads, latent_dim), bf16),
            pltpu.VMEM(value_up_weight.shape, bf16),
            pltpu.VMEM((2, count, latent_dim), bf16),
            pltpu.VMEM((2, count // 2, 2 * rope_dim), bf16),
            pltpu.VMEM((requests, heads, latent_dim + 128), f32),
            pltpu.VMEM((requests, own_heads, latent_dim + 128), f32),
            pltpu.VMEM((requests, own_heads, latent_dim), f32),
            pltpu.SemaphoreType.DMA((4,)),
            pltpu.SemaphoreType.DMA((2, 3, rank_count, chunk_count)),
            pltpu.SemaphoreType.DMA((2, rank_count, chunk_count)),
            pltpu.SemaphoreType.DMA((requests,)),
            pltpu.SemaphoreType.DMA((requests,)),
        ],
        compiler_params=pltpu.CompilerParams(
            collective_id=0, has_side_effects=True, vmem_limit_bytes=60 * 1024 * 1024
        ),
    )(
        table,
        lengths,
        cache_latent,
        rope_pairs,
        q_latent,
        value_up_weight,
        q_rope.reshape(requests, heads, rope_dim),
        new_entry.astype(f32),
    )


def local(*args):
    cache_latent = args[3]
    pool_bytes = lax.axis_size("dp") * cache_latent.size * 2
    fits = pool_bytes <= vmem_pool_limit and lax.axis_size("tp") == 2
    fits = fits and cache_latent.shape[0] % chunk_count == 0
    return (fused_local if fits else spread_local)(*args)


def solution(mesh):
    placed = (
        P(("pop", "dp"), None, None),
        P(("pop", "dp"), None),
        P(("pop", "dp"), None),
        P(("pop", "dp"), "tp", None),
        P(("pop", "dp"), "tp"),
        P(("pop", "dp"), None, None),
        P(("pop", "dp"), None),
        P(("pop", "dp")),
        P("tp", None, None),
    )
    return jax.shard_map(
        local, mesh=mesh, in_specs=placed, out_specs=P(("pop", "dp"), "tp"), check_vma=False
    )
```

```python
import functools

import jax
import jax.numpy as jnp
from jax import lax
from jax.experimental import pallas as pl
from jax.experimental.pallas import tpu as pltpu
from jax.sharding import PartitionSpec as P

softmax_scale = 192.0 ** (-0.5)
neg_fill = -1e30


def entry_places(src_flat, rank_count):
    onehot = (src_flat[:, None] == jnp.arange(rank_count, dtype=jnp.int32)[None, :]).astype(
        jnp.int32
    )
    before = jnp.cumsum(onehot, axis=0) - onehot
    return jnp.sum(before * onehot, axis=1)


def spread_local(
    q_latent,
    q_rope,
    new_entry,
    cache_latent,
    cache_rope,
    source_rank,
    slot_index,
    lengths,
    value_up_weight,
):
    rank_count = lax.axis_size("dp")
    lane_count = lax.axis_size("tp")
    my_lane = lax.axis_index("tp")
    requests, max_blocks = slot_index.shape
    run_len = cache_latent.shape[1]
    latent_dim = cache_latent.shape[2]
    heads = q_latent.shape[1]
    rope_dim = q_rope.shape[1] // heads
    entries = requests * max_blocks
    capacity = max(2, (entries * 5 + 4 * rank_count - 1) // (4 * rank_count))
    src_flat = source_rank.reshape(entries)
    slot_flat = slot_index.reshape(entries)
    places = entry_places(src_flat, rank_count)
    wanted = jnp.zeros((rank_count, capacity), jnp.int32).at[src_flat, places].set(slot_flat)
    asked_slots = lax.all_to_all(wanted, "dp", split_axis=0, concat_axis=0, tiled=True)
    send_latent = jnp.take(cache_latent, asked_slots, axis=0)
    send_rope = jnp.take(cache_rope, asked_slots, axis=0)
    got_latent, received_rotary_keys = (
        lax.all_to_all(send_latent, "dp", split_axis=0, concat_axis=0, tiled=True),
        lax.all_to_all(send_rope, "dp", split_axis=0, concat_axis=0, tiled=True),
    )
    where_from = src_flat * capacity + places
    keys_latent = jnp.take(
        got_latent.reshape(rank_count * capacity, run_len, latent_dim), where_from, axis=0
    )
    keys_latent = keys_latent.reshape(requests, max_blocks * run_len, latent_dim)
    keys_rope = jnp.take(
        received_rotary_keys.reshape(rank_count * capacity, run_len * rope_dim), where_from, axis=0
    )
    keys_rope = keys_rope.reshape(requests, max_blocks * run_len, rope_dim)
    query_rope = q_rope.reshape(requests, heads, rope_dim)
    scores = jnp.einsum("rhk,rnk->rhn", q_latent, keys_latent, preferred_element_type=jnp.float32)
    scores = (
        scores
        + jnp.einsum("rhd,rnd->rhn", query_rope, keys_rope, preferred_element_type=jnp.float32)
    ) * softmax_scale
    new_latent = new_entry[:, :latent_dim]
    incoming_rotary_key = new_entry[:, latent_dim:]
    new_score = jnp.einsum("rhk,rk->rh", q_latent, new_latent, preferred_element_type=jnp.float32)
    new_score = (
        new_score
        + jnp.einsum(
            "rhd,rd->rh", query_rope, incoming_rotary_key, preferred_element_type=jnp.float32
        )
    ) * softmax_scale
    slot_pos = jnp.arange(max_blocks * run_len, dtype=jnp.int32)
    positions = (
        slot_pos // run_len * (run_len * lane_count) + my_lane * run_len + slot_pos % run_len
    )
    in_range = (positions[None, :] < lengths[:, None])[:, None, :]
    is_first = my_lane == 0
    top_score = jnp.max(jnp.where(in_range, scores, neg_fill), axis=2)
    top_score = jnp.where(is_first, jnp.maximum(top_score, new_score), top_score)
    expo = jnp.where(in_range, jnp.exp(scores - top_score[:, :, None]), 0.0)
    numerator = jnp.einsum(
        "rhn,rnk->rhk", expo.astype(jnp.bfloat16), keys_latent, preferred_element_type=jnp.float32
    )
    denominator = jnp.sum(expo, axis=2)
    incoming_token_weight = jnp.where(is_first, jnp.exp(new_score - top_score), 0.0)
    numerator = (
        numerator
        + incoming_token_weight.astype(jnp.bfloat16).astype(jnp.float32)[:, :, None]
        * new_latent.astype(jnp.float32)[:, None, :]
    )
    denominator = denominator + incoming_token_weight
    overall = lax.pmax(top_score, "tp")
    factor = jnp.exp(top_score - overall)
    numer_sum, denom_sum = (
        lax.psum_scatter(numerator * factor[:, :, None], "tp", scatter_dimension=1, tiled=True),
        lax.psum_scatter(denominator * factor, "tp", scatter_dimension=1, tiled=True),
    )
    latent_output_rows = (numer_sum / denom_sum[:, :, None]).astype(jnp.bfloat16)
    value_projected_output = jnp.einsum(
        "wyc,yca->wya", latent_output_rows, value_up_weight, preferred_element_type=jnp.float32
    )
    return value_projected_output.reshape(requests, -1).astype(jnp.bfloat16)


MESH = pl.DeviceIdType.MESH
up, down, across = 0, 1, 2
chunk_count = 6
vmem_pool_limit = 24 * 1024 * 1024


def dot_nt(a, b):
    return lax.dot_general(a, b, (((1,), (1,)), ((), ())), preferred_element_type=jnp.float32)


def fused_kernel(
    depth,
    width,
    early,
    sources,
    slot_table,
    lengths,
    latent_hbm,
    rope_hbm,
    q_hbm,
    value_hbm,
    q_rope,
    new_entry,
    out,
    latent,
    rope,
    q_latent,
    value,
    keys,
    rope_keys,
    part,
    other,
    merged,
    q_low,
    q_high,
    fresh,
    local_sem,
    send_sem,
    recv_sem,
    pair_send,
    pair_recv,
):
    me = lax.axis_index("dp")
    lane = lax.axis_index("tp")
    z, y = me // width, me % width
    slots = latent_hbm.shape[0]
    run_len = latent_hbm.shape[1]
    latent_dim = latent_hbm.shape[2]
    requests, heads = q_hbm.shape[0], q_hbm.shape[1]
    rope_dim = q_rope.shape[1] // heads
    max_blocks = slot_table.shape[1]
    half = run_len // 2
    own_heads = heads // 2
    chunk = slots // chunk_count
    has_up, has_down = z + 1 < depth, z > 0

    own = pl.ds(me * slots, slots)
    local_copies = [
        pltpu.make_async_copy(latent_hbm, latent.at[own], local_sem.at[0]),
        pltpu.make_async_copy(rope_hbm, rope.at[own], local_sem.at[1]),
        pltpu.make_async_copy(q_hbm, q_latent, local_sem.at[2]),
        pltpu.make_async_copy(value_hbm, value, local_sem.at[3]),
    ]
    local_copies[0].start()
    local_copies[1].start()

    barrier = pltpu.get_barrier_semaphore()

    def greet(target):
        pl.semaphore_signal(barrier, inc=1, device_id=target, device_id_type=MESH)

    greet({"tp": 1 - lane})
    pl.when(has_up)(lambda: greet({"dp": me + width}))
    pl.when(has_down)(lambda: greet({"dp": me - width}))
    neighbours = 1 + has_up.astype(jnp.int32) + has_down.astype(jnp.int32)
    if width == 2:
        greet({"dp": z * width + 1 - y})
        neighbours = neighbours + 1
    pl.semaphore_wait(barrier, neighbours)
    local_copies[0].wait()
    local_copies[1].wait()

    def piece(n, origin, c, way):
        target = {up: me + width, down: me - width, across: z * width + 1 - y}[way]
        array = (latent, rope)[n]
        if n == 0:
            rows = pl.ds(origin * slots + c * chunk, chunk)
        elif c == 0:
            rows = pl.ds(origin * slots, early * chunk)
        else:
            rows = pl.ds(origin * slots + early * chunk, slots - early * chunk)
        return pltpu.make_async_remote_copy(
            src_ref=array.at[rows],
            dst_ref=array.at[rows],
            send_sem=send_sem.at[way, origin, c + n * chunk_count],
            recv_sem=recv_sem.at[origin, c + n * chunk_count],
            device_id={"dp": target},
            device_id_type=MESH,
        )

    def send(n, origin, c, way):
        piece(n, origin, c, way).start()

    def arrive(n, origin, c):
        piece(n, origin, c, up).wait_recv()

    def sent(n, origin, c, way):
        piece(n, origin, c, way).wait_send()

    def over(first, last, body):
        def step(c, carry):
            body(0, c)
            return carry

        lax.fori_loop(first, last, step, 0)
        body(1, 0 if first == 0 and early else 1)

    late = (early, chunk_count)

    def own_first(n, c):
        pl.when(has_up)(lambda: send(n, me, c, up))
        pl.when(has_down)(lambda: send(n, me, c, down))
        if width == 2:
            send(n, me, c, across)

    if width == 2:
        over(0, early, lambda n, c: send(n, me, c, across))
    over(*late, own_first)
    local_copies[2].start()
    local_copies[3].start()

    first_half = lax.broadcasted_iota(jnp.int32, (requests, 128), 1) < rope_dim

    def spread(p, carry):
        x = q_rope[:, pl.ds(pl.multiple_of(p * 128, 128), 128)].astype(jnp.float32)
        turned = pltpu.roll(x, rope_dim, 1)

        def put(array, head, values):
            array[:, pl.ds(head, 1), :] = values.reshape(requests, 1, 128)

        put(q_low, 2 * p, jnp.where(first_half, x, 0.0))
        put(q_high, 2 * p, jnp.where(first_half, 0.0, turned))
        put(q_low, 2 * p + 1, jnp.where(first_half, turned, 0.0))
        put(q_high, 2 * p + 1, jnp.where(first_half, 0.0, x))
        return carry

    lax.fori_loop(0, heads // 2, spread, 0)
    fresh[...] = jnp.zeros_like(fresh)
    fresh[:, 0 : latent_dim + rope_dim] = new_entry[...].astype(jnp.float32)

    def pass_on(t, columns, first, last, cross):
        def body(n, c):
            for column in columns:

                @pl.when(z >= t)
                def _():
                    origin = (z - t) * width + column
                    arrive(n, origin, c)
                    pl.when(has_up)(lambda: send(n, origin, c, up))
                    if cross:
                        send(n, origin, c, across)

                @pl.when(z + t < depth)
                def _():
                    origin = (z + t) * width + column
                    arrive(n, origin, c)
                    pl.when(has_down)(lambda: send(n, origin, c, down))
                    if cross:
                        send(n, origin, c, across)

        over(first, last, body)

    for t in range(1, depth):
        pass_on(t, (y,), *late, width == 2)

    if early:

        def own_last(n, c):
            partner = z * width + 1 - y
            arrive(n, partner, c)
            for origin in (me, partner):
                pl.when(has_up)(lambda: send(n, origin, c, up))
                pl.when(has_down)(lambda: send(n, origin, c, down))

        over(0, early, own_last)
        for t in range(1, depth):
            pass_on(t, (0, 1), 0, early, False)

    if width == 2:
        order = [(z + t) % depth for t in range(depth)]
        for place in order:
            over(*late, lambda n, c: arrive(n, place * width + 1 - y, c))

    local_copies[2].wait()
    local_copies[3].wait()

    def pair_copy(r):
        return pltpu.make_async_remote_copy(
            src_ref=part.at[r, pl.ds((1 - lane) * own_heads, own_heads)],
            dst_ref=other.at[r],
            send_sem=pair_send.at[r],
            recv_sem=pair_recv.at[r],
            device_id={"tp": 1 - lane},
            device_id_type=MESH,
        )

    count = max_blocks * run_len
    spot = lax.broadcasted_iota(jnp.int32, (heads, count), 1)
    in_half = spot % (count // 2)
    positions = (
        in_half // half * (2 * run_len) + lane * run_len + spot // (count // 2) * half + in_half % half
    )
    is_first = lane == 0
    stat_lane = lax.broadcasted_iota(jnp.int32, (heads, 128), 1)

    def attend(r, carry):
        side = r % 2
        pl.when(r > 0)(lambda: pair_copy(r - 1).start())
        for j in range(max_blocks):
            block = sources[r, j] * slots + slot_table[r, j]
            low = pl.ds(j * half, half)
            keys[side, low, :] = latent[block, 0:half, :]
            keys[side, pl.ds(count // 2 + j * half, half), :] = latent[block, half:run_len, :]
            rope_keys[side, low, :] = rope[block]
        q = q_latent[r]
        q_rot = q_low[r]
        rot = rope_keys[side]
        all_keys = keys[side]
        scores = dot_nt(q, all_keys)
        low_scores = dot_nt(q_rot.astype(jnp.bfloat16), rot)
        high_scores = dot_nt(q_high[r].astype(jnp.bfloat16), rot)
        scores = (scores + jnp.concatenate([low_scores, high_scores], axis=1)) * softmax_scale
        new = fresh[pl.ds(r, 1), :]
        new_latent = new[:, :latent_dim]
        new_score = jnp.sum(q.astype(jnp.float32) * new_latent, axis=1, keepdims=True)
        new_score = new_score + jnp.sum(
            q_rot * new[:, latent_dim : latent_dim + 128], axis=1, keepdims=True
        )
        new_score = new_score * softmax_scale
        in_range = positions < lengths[r]
        top = jnp.max(jnp.where(in_range, scores, neg_fill), axis=1, keepdims=True)
        top = jnp.where(is_first, jnp.maximum(top, new_score), top)
        expo = jnp.where(in_range, jnp.exp(scores - top), 0.0)
        weight = jnp.where(is_first, jnp.exp(new_score - top), 0.0)
        den = jnp.sum(expo, axis=1, keepdims=True) + weight
        num = jnp.dot(expo.astype(jnp.bfloat16), all_keys, preferred_element_type=jnp.float32)
        num = num + weight.astype(jnp.bfloat16).astype(jnp.float32) * new_latent
        part[r, :, 0:latent_dim] = num
        part[r, :, latent_dim : latent_dim + 128] = jnp.where(stat_lane < 64, top, den)
        return carry

    lax.fori_loop(0, requests, attend, 0, unroll=2)
    pair_copy(requests - 1).start()

    def merge(r, carry):
        pair_copy(r).wait_recv()
        a = part[r, pl.ds(pl.multiple_of(lane * own_heads, own_heads), own_heads), :]
        b = other[r]
        top_a, top_b = a[:, latent_dim : latent_dim + 1], b[:, latent_dim : latent_dim + 1]
        den_a, den_b = a[:, latent_dim + 64 : latent_dim + 65], b[:, latent_dim + 64 : latent_dim + 65]
        top = jnp.maximum(top_a, top_b)
        f_a, f_b = jnp.exp(top_a - top), jnp.exp(top_b - top)
        total = a[:, :latent_dim] * f_a + b[:, :latent_dim] * f_b
        merged[r] = total / (den_a * f_a + den_b * f_b)
        return carry

    lax.fori_loop(0, requests, merge, 0, unroll=2)

    value_dim = value.shape[2]

    def project(h, carry):
        rows = merged[:, pl.ds(h, 1), :].reshape(requests, latent_dim).astype(jnp.bfloat16)
        done = jnp.dot(rows, value[h], preferred_element_type=jnp.float32)
        out[:, pl.ds(pl.multiple_of(h * value_dim, value_dim), value_dim)] = done.astype(out.dtype)
        return carry

    lax.fori_loop(0, own_heads, project, 0, unroll=8)

    for place in range(depth):
        mine = place * width + y

        @pl.when(jnp.logical_and(place <= z, has_up))
        def _():
            over(*late, lambda n, c: sent(n, mine, c, up))
            for column in range(width) if early else ():
                over(0, early, lambda n, c: sent(n, place * width + column, c, up))

        @pl.when(jnp.logical_and(place >= z, has_down))
        def _():
            over(*late, lambda n, c: sent(n, mine, c, down))
            for column in range(width) if early else ():
                over(0, early, lambda n, c: sent(n, place * width + column, c, down))

        if width == 2:
            over(*late, lambda n, c: sent(n, mine, c, across))
    if early:
        over(0, early, lambda n, c: sent(n, me, c, across))

    def finish(r, carry):
        pair_copy(r).wait_send()
        return carry

    lax.fori_loop(0, requests, finish, 0)


def fused_local(
    q_latent,
    q_rope,
    new_entry,
    cache_latent,
    cache_rope,
    source_rank,
    slot_index,
    lengths,
    value_up_weight,
):
    rank_count = lax.axis_size("dp")
    width = 2 if rank_count % 2 == 0 else 1
    depth = rank_count // width
    early = chunk_count // 6 if width == 2 else 0
    requests, max_blocks = slot_index.shape
    slots, run_len, latent_dim = cache_latent.shape
    heads = q_latent.shape[1]
    rope_dim = q_rope.shape[1] // heads
    own_heads, _, value_dim = value_up_weight.shape
    half = run_len // 2
    rope_pairs = (
        cache_rope.reshape(slots, 2, half, rope_dim)
        .transpose(0, 2, 1, 3)
        .reshape(slots, half, 2 * rope_dim)
    )
    count = max_blocks * run_len
    bf16, f32 = jnp.bfloat16, jnp.float32
    smem = pl.BlockSpec(memory_space=pltpu.SMEM)
    vmem = pl.BlockSpec(memory_space=pltpu.VMEM)
    anywhere = pl.BlockSpec(memory_space=pl.ANY)
    return pl.pallas_call(
        functools.partial(fused_kernel, depth, width, early),
        out_shape=jax.ShapeDtypeStruct((requests, own_heads * value_dim), bf16),
        in_specs=[smem, smem, smem, anywhere, anywhere, anywhere, anywhere, vmem, vmem],
        out_specs=vmem,
        scratch_shapes=[
            pltpu.VMEM((rank_count * slots, run_len, latent_dim), bf16),
            pltpu.VMEM((rank_count * slots, half, 2 * rope_dim), bf16),
            pltpu.VMEM((requests, heads, latent_dim), bf16),
            pltpu.VMEM(value_up_weight.shape, bf16),
            pltpu.VMEM((2, count, latent_dim), bf16),
            pltpu.VMEM((2, count // 2, 2 * rope_dim), bf16),
            pltpu.VMEM((requests, heads, latent_dim + 128), f32),
            pltpu.VMEM((requests, own_heads, latent_dim + 128), f32),
            pltpu.VMEM((requests, own_heads, latent_dim), f32),
            pltpu.VMEM((requests, heads, 128), f32),
            pltpu.VMEM((requests, heads, 128), f32),
            pltpu.VMEM((requests, latent_dim + 128), f32),
            pltpu.SemaphoreType.DMA((4,)),
            pltpu.SemaphoreType.DMA((3, rank_count, chunk_count + 2)),
            pltpu.SemaphoreType.DMA((rank_count, chunk_count + 2)),
            pltpu.SemaphoreType.DMA((requests,)),
            pltpu.SemaphoreType.DMA((requests,)),
        ],
        compiler_params=pltpu.CompilerParams(
            collective_id=0, has_side_effects=True, vmem_limit_bytes=60 * 1024 * 1024
        ),
    )(
        source_rank.reshape(requests, max_blocks),
        slot_index,
        lengths,
        cache_latent,
        rope_pairs,
        q_latent,
        value_up_weight,
        q_rope,
        new_entry,
    )


def local(*args):
    cache_latent = args[3]
    pool_bytes = lax.axis_size("dp") * cache_latent.size * 2
    fits = pool_bytes <= vmem_pool_limit and lax.axis_size("tp") == 2
    fits = fits and cache_latent.shape[0] % chunk_count == 0 and args[1].shape[1] == args[0].shape[1] * 64
    return (fused_local if fits else spread_local)(*args)


def solution(mesh):
    placed = (
        P(("pop", "dp"), None, None),
        P(("pop", "dp"), None),
        P(("pop", "dp"), None),
        P(("pop", "dp"), "tp", None),
        P(("pop", "dp"), "tp"),
        P(("pop", "dp"), None, None),
        P(("pop", "dp"), None),
        P(("pop", "dp")),
        P("tp", None, None),
    )
    return jax.shard_map(
        local, mesh=mesh, in_specs=placed, out_specs=P(("pop", "dp"), "tp"), check_vma=False
    )
```
